32 devices in a mesh: tm: 8 (over y, x, core), space: 4 (over z).
Axes of the slice: x: 2, y: 2, z: 4, core: 2. Of those that a mesh axis runs over, the one named last changes fastest.
Arguments:
- c_state: float32 [8, 3, 2, 512, 1024], P('tm', None, None, 'space'), may hold values from -4 to 4
- init: float32 [3, 2, 512, 1024], P(None, None, 'space'), may hold values from -4 to 4
Outputs:
- new_c: float32 [8, 3, 2, 512, 1024], P('tm', None, None, 'space')
- residual: float32 [8, 3, 2, 512, 1024], P('tm', None, None, 'space')
The draws below stay inside these ranges and needn't reach their ends.
All inputs are finite; a program needn't handle non-finite values.
Results may differ from the reference program's by a relative error of at most 0.00019.
Values sent between devices are 32-bit elements; how exact they have to be, the bound alone decides.
A program may use at most 128 MiB of HBM per device.

```python
import jax
import jax.numpy as jnp
from jax import lax

NG = 1024
NGH = 512
CF = 2
SLABS = 8


def shard_levels(own_key, dims, shards, smallest, largest):
    gain = 1.0
    for axis_at, parts in shards:
        draws = jax.random.uniform(jax.random.fold_in(jax.random.fold_in(own_key, 6), axis_at), (parts,), jnp.float32, smallest / len(shards), largest / len(shards))
        gain = gain * jnp.repeat(jnp.exp(draws), dims[axis_at] // parts).reshape((-1,) + (1,) * (len(dims) - 1 - axis_at))
    return gain


def gaussian(rng, extent, deviation, reach, split=(), held_as=jnp.bfloat16):
    drawn = jax.random.normal(rng, extent, jnp.float32) * deviation
    if len(split) > 0:
        drawn = shard_levels(rng, extent, split, -0.22, 0.18) * drawn
    return jnp.clip(drawn, min=-reach, max=reach).astype(held_as)


def setup_inputs(seed: int = 0) -> dict:
    seeds = jax.random.split(jax.random.key(seed), 3)
    return {
        "c_state": gaussian(seeds[0], (SLABS, 3, 2, NGH, NG), 0.5, 4.0, ((0, 8), (3, 4)), jnp.float32),
        "init": gaussian(seeds[1], (3, 2, NGH, NG), 0.5, 4.0, ((2, 4),), jnp.float32),
    }


CORIOLIS = 1.0
HYPERDIFFUSION = 0.25
COURANT = 0.4

def times_imag(values):
    return jnp.stack([-values[..., 1, :, :], values[..., 0, :, :]], axis=-3)

def divide_imag(values):
    return jnp.stack([values[..., 1, :, :], -values[..., 0, :, :]], axis=-3)

def operator_m(x_wind, y_wind, tilted, wave_x, wave_y):
    return (CORIOLIS * y_wind - wave_x * tilted, -CORIOLIS * x_wind - wave_y * tilted, wave_x * x_wind + wave_y * y_wind)

def propagate(state, steps, wave_x, wave_y, grid_size):
    time_step = COURANT / grid_size
    squared = wave_x * wave_x + wave_y * wave_y
    frequency = jnp.sqrt(CORIOLIS * CORIOLIS + squared)
    ratio = squared / (0.25 * grid_size * grid_size)
    log_damp = -HYPERDIFFUSION * (ratio * ratio) * (ratio * ratio)
    phase_angle = frequency * (steps * time_step)
    first_coef = jnp.sin(phase_angle) / frequency
    second_coef = (1.0 - jnp.cos(phase_angle)) / (frequency * frequency)
    damping = jnp.exp(steps * log_damp)
    base = (state[..., 0, :, :, :], state[..., 1, :, :, :], times_imag(state[..., 2, :, :, :]))
    applied = operator_m(base[0], base[1], base[2], wave_x, wave_y)
    applied_twice = operator_m(applied[0], applied[1], applied[2], wave_x, wave_y)
    results = [(base[field_id] + first_coef * applied[field_id] + second_coef * applied_twice[field_id]) * damping for field_id in range(3)]
    return jnp.stack([results[0], results[1], divide_imag(results[2])], axis=-4)

def wave_tables():
    counter = jnp.arange(NG, dtype=jnp.int32)
    wave_x = jnp.where(counter < NG // 2, counter, counter - NG).astype(jnp.float32)
    wave_y = jnp.arange(NGH, dtype=jnp.int32).astype(jnp.float32)[:, None]
    keep_mask = ((jnp.abs(wave_x) <= NG // 3)[None, :] & (wave_y <= NG // 3)).astype(jnp.float32)
    return (wave_x, wave_y, keep_mask)

def to_grid(coefficients):
    values = lax.complex(coefficients[:, 0], coefficients[:, 1])
    along_x = jnp.fft.ifft(values, axis=-1) * NG
    lowest = (jnp.arange(NGH, dtype=jnp.int32) == 0)[:, None]
    along_x = lax.complex(jnp.real(along_x), jnp.where(lowest, jnp.zeros_like(jnp.imag(along_x)), jnp.imag(along_x)))
    padded = jnp.concatenate([along_x, jnp.zeros_like(along_x[:, :1])], axis=1)
    return jnp.transpose(jnp.fft.irfft(padded, n=NG, axis=1), (0, 2, 1))

def to_modes(physical):
    along_y = jnp.fft.rfft(physical, axis=2)[:, :, :NGH]
    spectrum = jnp.transpose(jnp.fft.fft(along_y, axis=1) / NG, (0, 2, 1))
    return jnp.stack([jnp.real(spectrum), jnp.imag(spectrum)], axis=1)

def fine_step(state, wave_x, wave_y, keep_mask):
    time_step = COURANT / NG
    x_wind, y_wind, height = (state[0], state[1], state[2])
    vortex = times_imag(wave_x * y_wind - wave_y * x_wind)
    physical = to_grid(jnp.stack([x_wind, y_wind, height, vortex]))
    east_flow, north_flow, depth_field, spin_field = (physical[0], physical[1], physical[2], physical[3])
    products = jnp.stack([spin_field * north_flow, spin_field * east_flow, 0.5 * (east_flow * east_flow + north_flow * north_flow), depth_field * east_flow, depth_field * north_flow])
    modes = to_modes(products)
    tend_x = modes[0] - times_imag(wave_x * modes[2])
    tend_y = -modes[1] - times_imag(wave_y * modes[2])
    tend_h = -times_imag(wave_x * modes[3] + wave_y * modes[4])
    tendency = jnp.stack([tend_x, tend_y, tend_h]) * keep_mask
    return propagate(state + time_step * tendency, 1.0, wave_x, wave_y, NG)

def reference(c_state, init):
    wave_x, wave_y, keep_mask = wave_tables()
    previous = jnp.concatenate([init[None], c_state[:-1]], axis=0)

    def run_slab(start_state):
        current = start_state
        for repeat in range(CF):
            current = fine_step(current, wave_x, wave_y, keep_mask)
        return current
    ends = lax.map(run_slab, previous)
    residual = ends - c_state
    offsets = ends - propagate(previous, float(CF), wave_x, wave_y, NG)

    def advance(carried, offset):
        updated = propagate(carried, float(CF), wave_x, wave_y, NG) + offset
        return (updated, updated)
    last_state, new_c = lax.scan(advance, init, offsets)
    return (new_c, residual)
```

```python
import math

import jax
import jax.numpy as jnp
import numpy as np
from jax import lax
from jax.experimental import pallas as pl
from jax.experimental.pallas import tpu as pltpu
from jax.sharding import Mesh, PartitionSpec as P

CF = 2
CORIOLIS = 1.0
HYPERDIFFUSION = 0.25
COURANT = 0.4
RADIX = 8
SLAB = ("ta", "core")
SPACE = ("zh", "zl")
GROUP = ("core", "zl")
EVERY = ("ta", "core", "zh", "zl")


def split_pair(values):
    high = values.astype(jnp.bfloat16)
    return high, (values - high.astype(jnp.float32)).astype(jnp.bfloat16)


def table_pair(values):
    high = lax.reduce_precision(values, 8, 7)
    return jnp.stack([high, values - high]).astype(jnp.bfloat16)


def dot3(left, right):
    def one(a, b):
        return jnp.dot(a, b, preferred_element_type=jnp.float32)

    return one(left[0], right[0]) + (one(left[0], right[1]) + one(left[1], right[0]))


def small_fft(parts, sign):
    count = len(parts)
    if count == 1:
        return parts
    even = small_fft(parts[0::2], sign)
    odd = small_fft(parts[1::2], sign)
    low, high = [], []
    for k in range(count // 2):
        re, im = odd[k]
        if k == 0:
            tr, ti = re, im
        elif 4 * k == count:
            tr, ti = (-im, re) if sign > 0 else (im, -re)
        else:
            c = math.cos(2.0 * math.pi * k / count)
            s = sign * math.sin(2.0 * math.pi * k / count)
            tr, ti = re * c - im * s, re * s + im * c
        low.append((even[k][0] + tr, even[k][1] + ti))
        high.append((even[k][0] - tr, even[k][1] - ti))
    return low + high


def lane_tables(grid_size, sign):
    lanes = grid_size // RADIX
    n = np.arange(lanes)
    angle = 2.0 * np.pi * (n[:, None] * n[None, :] % lanes) / lanes
    c, s = np.cos(angle), sign * np.sin(angle)
    full = jnp.asarray(np.block([[c, s], [-s, c]]), jnp.float32)
    turn = 2.0 * np.pi * (np.arange(RADIX)[:, None] * n[None, :]) / grid_size
    twiddle = np.stack([np.cos(turn), sign * np.sin(turn)]).astype(np.float32)
    return table_pair(full), jnp.asarray(twiddle)


def prop_factors(steps, wave_x, wave_y, grid_size):
    time_step = COURANT / grid_size
    squared = wave_x * wave_x + wave_y * wave_y
    frequency = jnp.sqrt(CORIOLIS * CORIOLIS + squared)
    ratio = squared / (0.25 * grid_size * grid_size)
    log_damp = -HYPERDIFFUSION * (ratio * ratio) * (ratio * ratio)
    phase_angle = frequency * (steps * time_step)
    first_coef = jnp.sin(phase_angle) / frequency
    second_coef = (1.0 - jnp.cos(phase_angle)) / (frequency * frequency)
    damping = jnp.exp(steps * log_damp)
    return jnp.stack([first_coef, second_coef, damping])


def apply_parts(state, factors, kx, ky):
    first, second, damp = factors
    (xr, xi), (yr, yi), (hr, hi) = state
    done = []
    for x, y, p in ((xr, yr, -hi), (xi, yi, hr)):
        m1 = CORIOLIS * y - kx * p
        m2 = -CORIOLIS * x - ky * p
        m3 = kx * x + ky * y
        n1 = CORIOLIS * m2 - kx * m3
        n2 = -CORIOLIS * m1 - ky * m3
        n3 = kx * m1 + ky * m2
        done.append(
            (
                (x + first * m1 + second * n1) * damp,
                (y + first * m2 + second * n2) * damp,
                (p + first * m3 + second * n3) * damp,
            )
        )
    real, imag = done
    return ((real[0], imag[0]), (real[1], imag[1]), (imag[2], -real[2]))


def inverse_kernel(state_ref, kx_ref, ky_ref, mat_ref, tw_ref, out_ref):
    kx, ky = kx_ref[...], ky_ref[...]
    lanes = mat_ref.shape[1] // 2
    chunk = out_ref.shape[4]
    rows = ky.shape[0]
    matrix = (mat_ref[0], mat_ref[1])
    for f in range(4):
        if f < 3:
            re, im = state_ref[f, 0], state_ref[f, 1]
        else:
            re = ky * state_ref[0, 1] - kx * state_ref[1, 1]
            im = kx * state_ref[1, 0] - ky * state_ref[0, 0]
        parts = [
            (re[:, n * lanes : (n + 1) * lanes], im[:, n * lanes : (n + 1) * lanes])
            for n in range(RADIX)
        ]
        parts = small_fft(parts, 1.0)
        turned = []
        for k, (a, b) in enumerate(parts):
            if k > 0:
                c, s = tw_ref[0, k : k + 1], tw_ref[1, k : k + 1]
                a, b = a * c - b * s, a * s + b * c
            turned.append(jnp.concatenate([a, b], axis=1))
        made = dot3(split_pair(jnp.concatenate(turned, axis=0)), matrix)
        for k in range(RADIX):
            for c in range(2):
                block = made[k * rows : (k + 1) * rows, c * lanes : (c + 1) * lanes]
                if chunk >= lanes:
                    g, at = divmod(k * lanes, chunk)
                    out_ref[g, f, c, :, at : at + lanes] = block
                else:
                    per = lanes // chunk
                    for i in range(per):
                        out_ref[k * per + i, f, c] = block[:, i * chunk : (i + 1) * chunk]


def inverse_x(state, tables):
    _, _, rows, grid_size = state.shape
    group = tables["group"]
    chunk = grid_size // group
    step = min(rows, 32)
    mat, tw = tables["inv_x"]
    return pl.pallas_call(
        inverse_kernel,
        grid=(rows // step,),
        in_specs=[
            pl.BlockSpec((3, 2, step, grid_size), lambda i: (0, 0, i, 0)),
            pl.BlockSpec((1, grid_size), lambda i: (0, 0)),
            pl.BlockSpec((step, 1), lambda i: (i, 0)),
            pl.BlockSpec(mat.shape, lambda i: (0, 0, 0)),
            pl.BlockSpec(tw.shape, lambda i: (0, 0, 0)),
        ],
        out_specs=pl.BlockSpec((group, 4, 2, step, chunk), lambda i: (0, 0, 0, i, 0)),
        out_shape=jax.ShapeDtypeStruct((group, 4, 2, rows, chunk), jnp.float32),
        name="inverse_x",
    )(state, tables["kx"], tables["ky"], mat, tw)


def middle_kernel(data_ref, inv_ref, fwd_ref, out_ref, high, low, total):
    at = pl.program_id(0)
    group, _, _, rows, chunk = data_ref.shape
    kept = out_ref.shape[3]

    @pl.when(at == 0)
    def _():
        for f in range(4):
            a, b = split_pair(data_ref[:, f].reshape(group * 2 * rows, chunk))
            high[f], low[f] = a, b

    u, v, h, z = (
        dot3((inv_ref[0], inv_ref[1]), (high[f], low[f])) for f in range(4)
    )
    products = (z * v, z * u, 0.5 * (u * u + v * v), h * u, h * v)
    for f in range(5):
        term = dot3((fwd_ref[0], fwd_ref[1]), split_pair(products[f]))

        @pl.when(at == 0)
        def _():
            total[f] = term

        @pl.when(at > 0)
        def _():
            total[f] = total[f] + term

    @pl.when(at == pl.num_programs(0) - 1)
    def _():
        for f in range(5):
            out_ref[:, f] = total[f].reshape(group, 2, kept, chunk)


def middle(data, tables):
    group, _, _, rows, chunk = data.shape
    inv, fwd = tables["inv_y"], tables["fwd_y"]
    grid_size = inv.shape[1]
    kept = fwd.shape[1] // (2 * group)
    step = grid_size // 4
    return pl.pallas_call(
        middle_kernel,
        grid=(grid_size // step,),
        in_specs=[
            pl.BlockSpec(data.shape, lambda i: (0, 0, 0, 0, 0)),
            pl.BlockSpec((2, step, inv.shape[2]), lambda i: (0, i, 0)),
            pl.BlockSpec((2, fwd.shape[1], step), lambda i: (0, 0, i)),
        ],
        out_specs=pl.BlockSpec((group, 5, 2, kept, chunk), lambda i: (0, 0, 0, 0, 0)),
        out_shape=jax.ShapeDtypeStruct((group, 5, 2, kept, chunk), jnp.float32),
        scratch_shapes=[
            pltpu.VMEM((4, group * 2 * rows, chunk), jnp.bfloat16),
            pltpu.VMEM((4, group * 2 * rows, chunk), jnp.bfloat16),
            pltpu.VMEM((5, group * 2 * kept, chunk), jnp.float32),
        ],
        compiler_params=pltpu.CompilerParams(vmem_limit_bytes=56 * 1024 * 1024),
        name="middle",
    )(data, inv, fwd)


def forward_kernel(kept_steps, dt, limit, data_ref, state_ref, fac_ref, kx_ref, ky_ref, mat_ref, tw_ref, out_ref):
    kx, ky = kx_ref[...], ky_ref[...]
    group, chunk = data_ref.shape[0], data_ref.shape[4]
    rows = ky.shape[0]
    lanes = mat_ref.shape[1] // 2
    factors = (fac_ref[0], fac_ref[1], fac_ref[2])
    state = tuple((state_ref[f, 0], state_ref[f, 1]) for f in range(3))

    def put(values):
        for f in range(3):
            for c in range(2):
                out_ref[f, c] = values[f][c]

    @pl.when(pl.program_id(0) >= kept_steps)
    def _():
        put(apply_parts(state, factors, kx, ky))

    @pl.when(pl.program_id(0) < kept_steps)
    def _():
        matrix = (mat_ref[0], mat_ref[1])

        def piece(f, c, k):
            if chunk >= lanes:
                g, at = divmod(k * lanes, chunk)
                return data_ref[g, f, c, :, at : at + lanes]
            per = lanes // chunk
            return jnp.concatenate([data_ref[k * per + i, f, c] for i in range(per)], axis=1)

        stacked = jnp.concatenate(
            [
                jnp.concatenate([piece(f, 0, k), piece(f, 1, k)], axis=1)
                for f in range(5)
                for k in range(RADIX)
            ],
            axis=0,
        )
        made = dot3(split_pair(stacked), matrix)
        modes = []
        for f in range(5):
            parts = []
            for k in range(RADIX):
                start = (f * RADIX + k) * rows
                a = made[start : start + rows, :lanes]
                b = made[start : start + rows, lanes:]
                if k > 0:
                    c, s = tw_ref[0, k : k + 1], tw_ref[1, k : k + 1]
                    a, b = a * c - b * s, a * s + b * c
                parts.append((a, b))
            parts = small_fft(parts, -1.0)
            modes.append(
                (
                    jnp.concatenate([p[0] for p in parts], axis=1),
                    jnp.concatenate([p[1] for p in parts], axis=1),
                )
            )
        (ar, ai), (br, bi), (kr, ki), (pr, pi), (qr, qi) = modes
        keep = jnp.where((jnp.abs(kx) <= limit) & (ky <= limit), dt, 0.0)
        (xr, xi), (yr, yi), (hr, hi) = state
        put(
            apply_parts(
                (
                    (xr + keep * (ar + kx * ki), xi + keep * (ai - kx * kr)),
                    (yr + keep * (ky * ki - br), yi - keep * (bi + ky * kr)),
                    (hr + keep * (kx * pi + ky * qi), hi - keep * (kx * pr + ky * qr)),
                ),
                factors,
                kx,
                ky,
            )
        )


def forward_x(data, state, tables):
    group, _, _, kept, chunk = data.shape
    _, _, rows, grid_size = state.shape
    step = 8
    kept_steps = kept // step
    mat, tw = tables["fwd_x"]

    def kernel(*refs):
        forward_kernel(kept_steps, COURANT / grid_size, float(grid_size // 3), *refs)

    return pl.pallas_call(
        kernel,
        grid=(rows // step,),
        in_specs=[
            pl.BlockSpec(
                (group, 5, 2, step, chunk),
                lambda i: (0, 0, 0, jnp.minimum(i, kept_steps - 1), 0),
            ),
            pl.BlockSpec((3, 2, step, grid_size), lambda i: (0, 0, i, 0)),
            pl.BlockSpec((3, step, grid_size), lambda i: (0, i, 0)),
            pl.BlockSpec((1, grid_size), lambda i: (0, 0)),
            pl.BlockSpec((step, 1), lambda i: (i, 0)),
            pl.BlockSpec(mat.shape, lambda i: (0, 0, 0)),
            pl.BlockSpec(tw.shape, lambda i: (0, 0, 0)),
        ],
        out_specs=pl.BlockSpec((3, 2, step, grid_size), lambda i: (0, 0, i, 0)),
        out_shape=jax.ShapeDtypeStruct(state.shape, jnp.float32),
        name="forward_x",
    )(data, state, tables["factors"], tables["kx"], tables["ky"], mat, tw)


def scan_kernel(data_ref, fac_ref, kx_ref, ky_ref, out_ref):
    kx, ky = kx_ref[...], ky_ref[...]
    factors = (fac_ref[0], fac_ref[1], fac_ref[2])
    carried = None
    for k in range(data_ref.shape[0]):
        new = tuple((data_ref[k, f, 0], data_ref[k, f, 1]) for f in range(3))
        if carried is not None:
            moved = apply_parts(carried, factors, kx, ky)
            new = tuple(
                (moved[f][0] + new[f][0], moved[f][1] + new[f][1]) for f in range(3)
            )
        for f in range(3):
            for c in range(2):
                out_ref[k, f, c] = new[f][c]
        carried = new


def slab_scan(data, factors, kx, ky):
    slabs, _, _, rows, grid_size = data.shape
    step = grid_size // 8
    return pl.pallas_call(
        scan_kernel,
        grid=(grid_size // step,),
        in_specs=[
            pl.BlockSpec((slabs, 3, 2, rows, step), lambda i: (0, 0, 0, 0, i)),
            pl.BlockSpec((3, rows, step), lambda i: (0, 0, i)),
            pl.BlockSpec((1, step), lambda i: (0, i)),
            pl.BlockSpec((rows, 1), lambda i: (0, 0)),
        ],
        out_specs=pl.BlockSpec((slabs, 3, 2, rows, step), lambda i: (0, 0, 0, 0, i)),
        out_shape=jax.ShapeDtypeStruct(data.shape, jnp.float32),
        name="slab_scan",
    )(data, factors, kx, ky)


def make_tables(grid_size, rows, group, mine):
    counter = jnp.arange(grid_size, dtype=jnp.int32)
    kx = jnp.where(counter < grid_size // 2, counter, counter - grid_size).astype(jnp.float32)[None]
    ky = (group * jnp.arange(rows, dtype=jnp.int32) + mine).astype(jnp.float32)[:, None]
    kept = -(-(grid_size // 3 + 1) // group)
    kept = min(rows, -(-kept // 8) * 8)
    freq = (
        group * jnp.arange(rows, dtype=jnp.int32)[None]
        + jnp.arange(group, dtype=jnp.int32)[:, None]
    )
    turns = freq[:, :, None] * counter % grid_size
    angle = 2.0 * math.pi / grid_size * turns.astype(jnp.float32)
    waves = jnp.stack([jnp.cos(angle), -jnp.sin(angle)], axis=1)
    forward = (waves[:, :, :kept] / grid_size).reshape(group * 2 * kept, grid_size)
    turns = counter[:, None, None] * freq[None] % grid_size
    angle = 2.0 * math.pi / grid_size * turns.astype(jnp.float32)
    weight = jnp.where(freq == 0, 1.0, 2.0).astype(jnp.float32) / grid_size
    inverse = jnp.stack([weight * jnp.cos(angle), -weight * jnp.sin(angle)], axis=2)
    inverse = inverse.reshape(grid_size, group * 2 * rows)
    return {
        "group": group,
        "kx": kx,
        "ky": ky,
        "inv_y": table_pair(inverse),
        "fwd_y": table_pair(forward),
        "inv_x": lane_tables(grid_size, 1.0),
        "fwd_x": lane_tables(grid_size, -1.0),
        "factors": prop_factors(1.0, kx, ky, grid_size),
    }


def fine_step(state, tables):
    rotated = inverse_x(state, tables)
    rotated = lax.all_to_all(rotated, GROUP, split_axis=0, concat_axis=0, tiled=True)
    partial_y = middle(rotated, tables)
    partial_y = lax.all_to_all(partial_y, GROUP, split_axis=0, concat_axis=0, tiled=True)
    return forward_x(partial_y, state, tables)


def gathered(values, slabs, group, back):
    _, _, rows, grid_size = values.shape
    half = group // 2
    ident = lax.axis_index(SPACE)
    own = lax.axis_index(GROUP)
    per = rows // group
    shift = 0 if back else 1
    if back:
        pieces = values.reshape(3, 2, group, per, grid_size)
    else:
        pieces = values.reshape(3, 2, per, group, grid_size).transpose(3, 0, 1, 2, 4)

    landed = []
    for turn in range(group):
        links = []
        for slab in range(slabs):
            to_slab = (slab + shift) % slabs
            for z in range(group):
                q = (z + turn) % group
                far = (((to_slab // 2) * 2 + q // half) * 2 + to_slab % 2) * half + q % half
                near = slab * group + z
                links.append((far, near) if back else (near, far))
        if back:
            piece = lax.dynamic_index_in_dim(pieces, (own - turn) % group, 2, keepdims=False)
        else:
            piece = lax.dynamic_index_in_dim(pieces, (ident + turn) % group, 0, keepdims=False)
        landed.append(lax.ppermute(piece, EVERY, links))
    stacked = jnp.stack(landed)
    order = jnp.arange(group, dtype=jnp.int32)
    if back:
        stacked = jnp.take(stacked, (order - ident) % group, axis=0)
        return stacked.transpose(1, 2, 3, 0, 4).reshape(values.shape)
    stacked = jnp.take(stacked, (own - order) % group, axis=0)
    return stacked.transpose(1, 2, 0, 3, 4).reshape(values.shape)


def shards(c_state, init):
    rows, grid_size = c_state.shape[3:]
    group = lax.axis_size(SPACE)
    slabs = lax.axis_size(SLAB)
    own_slab = lax.axis_index(SLAB)
    tables = make_tables(grid_size, rows, group, lax.axis_index(GROUP))
    current = c_state[0]
    current = gathered(jnp.where(own_slab == slabs - 1, init, current), slabs, group, False)
    for _ in range(CF):
        current = fine_step(current, tables)
    residual = gathered(current, slabs, group, True) - c_state[0]

    per = rows // slabs
    start = lax.axis_index(SPACE) * rows + own_slab * per
    ky = (start + jnp.arange(per, dtype=jnp.int32)).astype(jnp.float32)[:, None]
    coarse = prop_factors(float(CF), tables["kx"], ky, grid_size)
    split = residual.reshape(3, 2, slabs, per, grid_size).transpose(2, 0, 1, 3, 4)
    split = lax.all_to_all(split, SLAB, split_axis=0, concat_axis=0, tiled=True)
    split = slab_scan(split, coarse, tables["kx"], ky)
    split = lax.all_to_all(split, SLAB, split_axis=0, concat_axis=0, tiled=True)
    moved = split.transpose(1, 2, 0, 3, 4).reshape(residual.shape)
    return (c_state + moved[None], residual[None])


def solution(mesh):
    slabs, space = mesh.devices.shape
    fine = Mesh(mesh.devices.reshape(slabs // 2, 2, 2, space // 2), EVERY)
    spec = P(SLAB, None, None, SPACE, None)
    return jax.shard_map(
        shards,
        mesh=fine,
        in_specs=(spec, P(None, None, SPACE, None)),
        out_specs=(spec, spec),
        check_vma=False,
    )
```

```python
import math

import jax
import jax.numpy as jnp
import numpy as np
from jax import lax
from jax.experimental import pallas as pl
from jax.experimental.pallas import tpu as pltpu
from jax.sharding import Mesh, PartitionSpec as P

CF = 2
CORIOLIS = 1.0
HYPERDIFFUSION = 0.25
COURANT = 0.4
RADIX = 8
STREAMS = 2
SLAB = ("ta", "core")
SPACE = ("zh", "zl")
GROUP = ("core", "zl")
EVERY = ("ta", "core", "zh", "zl")


def split_pair(values):
    high = values.astype(jnp.bfloat16)
    return high, (values - high.astype(jnp.float32)).astype(jnp.bfloat16)


def table_pair(values):
    high = lax.reduce_precision(values, 8, 7)
    return jnp.stack([high, values - high]).astype(jnp.bfloat16)


def dot3(left, right):
    def one(a, b):
        return jnp.dot(a, b, preferred_element_type=jnp.float32)

    return one(left[0], right[0]) + (one(left[0], right[1]) + one(left[1], right[0]))


def small_fft(parts, sign):
    count = len(parts)
    if count == 1:
        return parts
    even = small_fft(parts[0::2], sign)
    odd = small_fft(parts[1::2], sign)
    low, high = [], []
    for k in range(count // 2):
        re, im = odd[k]
        if k == 0:
            tr, ti = re, im
        elif 4 * k == count:
            tr, ti = (-im, re) if sign > 0 else (im, -re)
        else:
            c = math.cos(2.0 * math.pi * k / count)
            s = sign * math.sin(2.0 * math.pi * k / count)
            tr, ti = re * c - im * s, re * s + im * c
        low.append((even[k][0] + tr, even[k][1] + ti))
        high.append((even[k][0] - tr, even[k][1] - ti))
    return low + high


def lane_tables(grid_size, sign):
    lanes = grid_size // RADIX
    n = np.arange(lanes)
    angle = 2.0 * np.pi * (n[:, None] * n[None, :] % lanes) / lanes
    c, s = np.cos(angle), sign * np.sin(angle)
    full = jnp.asarray(np.block([[c, s], [-s, c]]), jnp.float32)
    turn = 2.0 * np.pi * (np.arange(RADIX)[:, None] * n[None, :]) / grid_size
    twiddle = np.stack([np.cos(turn), sign * np.sin(turn)]).astype(np.float32)
    return table_pair(full), jnp.asarray(twiddle)


def prop_factors(steps, wave_x, wave_y, grid_size):
    time_step = COURANT / grid_size
    squared = wave_x * wave_x + wave_y * wave_y
    frequency = jnp.sqrt(CORIOLIS * CORIOLIS + squared)
    ratio = squared / (0.25 * grid_size * grid_size)
    log_damp = -HYPERDIFFUSION * (ratio * ratio) * (ratio * ratio)
    phase_angle = frequency * (steps * time_step)
    first_coef = jnp.sin(phase_angle) / frequency
    second_coef = (1.0 - jnp.cos(phase_angle)) / (frequency * frequency)
    damping = jnp.exp(steps * log_damp)
    return jnp.stack([first_coef, second_coef, damping])


def apply_parts(state, factors, kx, ky):
    first, second, damp = factors
    (xr, xi), (yr, yi), (hr, hi) = state
    done = []
    for x, y, p in ((xr, yr, -hi), (xi, yi, hr)):
        m1 = CORIOLIS * y - kx * p
        m2 = -CORIOLIS * x - ky * p
        m3 = kx * x + ky * y
        n1 = CORIOLIS * m2 - kx * m3
        n2 = -CORIOLIS * m1 - ky * m3
        n3 = kx * m1 + ky * m2
        done.append(
            (
                (x + first * m1 + second * n1) * damp,
                (y + first * m2 + second * n2) * damp,
                (p + first * m3 + second * n3) * damp,
            )
        )
    real, imag = done
    return ((real[0], imag[0]), (real[1], imag[1]), (imag[2], -real[2]))


def inverse_kernel(state_ref, kx_ref, ky_ref, mat_ref, tw_ref, *outs):
    kx, ky = kx_ref[...], ky_ref[...]
    lanes = mat_ref.shape[1] // 2
    width = outs[0].shape[4]
    chunk = width * len(outs)
    rows = ky.shape[0]
    matrix = (mat_ref[0], mat_ref[1])
    for f in range(4):
        if f < 3:
            re, im = state_ref[f, 0], state_ref[f, 1]
        else:
            re = ky * state_ref[0, 1] - kx * state_ref[1, 1]
            im = kx * state_ref[1, 0] - ky * state_ref[0, 0]
        parts = [
            (re[:, n * lanes : (n + 1) * lanes], im[:, n * lanes : (n + 1) * lanes])
            for n in range(RADIX)
        ]
        parts = small_fft(parts, 1.0)
        turned = []
        for k, (a, b) in enumerate(parts):
            if k > 0:
                c, s = tw_ref[0, k : k + 1], tw_ref[1, k : k + 1]
                a, b = a * c - b * s, a * s + b * c
            turned.append(jnp.concatenate([a, b], axis=1))
        made = dot3(split_pair(jnp.concatenate(turned, axis=0)), matrix)
        for k in range(RADIX):
            for c in range(2):
                block = made[k * rows : (k + 1) * rows, c * lanes : (c + 1) * lanes]
                if chunk >= lanes:
                    g, at = divmod(k * lanes, chunk)
                    o, at = divmod(at, width)
                    outs[o][g, f, c, :, at : at + lanes] = block
                else:
                    per = lanes // chunk
                    for i in range(per):
                        outs[0][k * per + i, f, c] = block[:, i * chunk : (i + 1) * chunk]


def inverse_x(state, tables):
    _, _, rows, grid_size = state.shape
    group = tables["group"]
    chunk = grid_size // group
    lanes = grid_size // RADIX
    count = 2 if chunk % (2 * lanes) == 0 else 1
    width = chunk // count
    step = min(rows, 32)
    mat, tw = tables["inv_x"]
    return pl.pallas_call(
        inverse_kernel,
        grid=(rows // step,),
        in_specs=[
            pl.BlockSpec((3, 2, step, grid_size), lambda i: (0, 0, i, 0)),
            pl.BlockSpec((1, grid_size), lambda i: (0, 0)),
            pl.BlockSpec((step, 1), lambda i: (i, 0)),
            pl.BlockSpec(mat.shape, lambda i: (0, 0, 0)),
            pl.BlockSpec(tw.shape, lambda i: (0, 0, 0)),
        ],
        out_specs=[pl.BlockSpec((group, 4, 2, step, width), lambda i: (0, 0, 0, i, 0))] * count,
        out_shape=[jax.ShapeDtypeStruct((group, 4, 2, rows, width), jnp.float32)] * count,
        name="inverse_x",
    )(state, tables["kx"], tables["ky"], mat, tw)


def middle_kernel(data_ref, inv_ref, fwd_ref, out_ref, high, low, total):
    at = pl.program_id(0)
    group, _, _, rows, chunk = data_ref.shape
    kept = out_ref.shape[3]

    @pl.when(at == 0)
    def _():
        for f in range(4):
            a, b = split_pair(data_ref[:, f].reshape(group * 2 * rows, chunk))
            high[:, f * chunk : (f + 1) * chunk] = a
            low[:, f * chunk : (f + 1) * chunk] = b

    made = dot3((inv_ref[0], inv_ref[1]), (high[...], low[...]))
    u, v, h, z = (made[:, f * chunk : (f + 1) * chunk] for f in range(4))
    products = (z * v, z * u, 0.5 * (u * u + v * v), h * u, h * v)
    term = dot3((fwd_ref[0], fwd_ref[1]), split_pair(jnp.concatenate(products, axis=1)))

    @pl.when(at == 0)
    def _():
        total[...] = term

    @pl.when(at > 0)
    def _():
        total[...] = total[...] + term

    @pl.when(at == pl.num_programs(0) - 1)
    def _():
        for f in range(5):
            field = total[:, f * chunk : (f + 1) * chunk]
            out_ref[:, f] = field.reshape(group, 2, kept, chunk)


def middle(data, tables):
    group, _, _, rows, chunk = data.shape
    inv, fwd = tables["inv_y"], tables["fwd_y"]
    grid_size = inv.shape[1]
    kept = fwd.shape[1] // (2 * group)
    step = grid_size // 4
    return pl.pallas_call(
        middle_kernel,
        grid=(grid_size // step,),
        in_specs=[
            pl.BlockSpec(data.shape, lambda i: (0, 0, 0, 0, 0)),
            pl.BlockSpec((2, step, inv.shape[2]), lambda i: (0, i, 0)),
            pl.BlockSpec((2, fwd.shape[1], step), lambda i: (0, 0, i)),
        ],
        out_specs=pl.BlockSpec((group, 5, 2, kept, chunk), lambda i: (0, 0, 0, 0, 0)),
        out_shape=jax.ShapeDtypeStruct((group, 5, 2, kept, chunk), jnp.float32),
        scratch_shapes=[
            pltpu.VMEM((group * 2 * rows, 4 * chunk), jnp.bfloat16),
            pltpu.VMEM((group * 2 * rows, 4 * chunk), jnp.bfloat16),
            pltpu.VMEM((group * 2 * kept, 5 * chunk), jnp.float32),
        ],
        compiler_params=pltpu.CompilerParams(vmem_limit_bytes=56 * 1024 * 1024),
        cost_estimate=pl.CostEstimate(
            flops=6 * grid_size * chunk * (4 * inv.shape[2] + 5 * fwd.shape[1]),
            bytes_accessed=4 * (inv.size + fwd.size + 2 * data.size),
            transcendentals=0,
        ),
        name="middle",
    )(data, inv, fwd)


def forward_kernel(kept_steps, dt, limit, datas, state_ref, fac_ref, kx_ref, ky_ref, mat_ref, tw_ref, out_ref):
    kx, ky = kx_ref[...], ky_ref[...]
    group, width = datas[0].shape[0], datas[0].shape[4]
    chunk = width * len(datas)
    rows = ky.shape[0]
    lanes = mat_ref.shape[1] // 2
    factors = (fac_ref[0], fac_ref[1], fac_ref[2])
    state = tuple((state_ref[f, 0], state_ref[f, 1]) for f in range(3))

    def put(values):
        for f in range(3):
            for c in range(2):
                out_ref[f, c] = values[f][c]

    @pl.when(pl.program_id(0) >= kept_steps)
    def _():
        put(apply_parts(state, factors, kx, ky))

    @pl.when(pl.program_id(0) < kept_steps)
    def _():
        matrix = (mat_ref[0], mat_ref[1])

        def piece(f, c, k):
            if chunk >= lanes:
                g, at = divmod(k * lanes, chunk)
                o, at = divmod(at, width)
                return datas[o][g, f, c, :, at : at + lanes]
            per = lanes // chunk
            return jnp.concatenate([datas[0][k * per + i, f, c] for i in range(per)], axis=1)

        stacked = jnp.concatenate(
            [
                jnp.concatenate([piece(f, 0, k), piece(f, 1, k)], axis=1)
                for f in range(5)
                for k in range(RADIX)
            ],
            axis=0,
        )
        made = dot3(split_pair(stacked), matrix)
        modes = []
        for f in range(5):
            parts = []
            for k in range(RADIX):
                start = (f * RADIX + k) * rows
                a = made[start : start + rows, :lanes]
                b = made[start : start + rows, lanes:]
                if k > 0:
                    c, s = tw_ref[0, k : k + 1], tw_ref[1, k : k + 1]
                    a, b = a * c - b * s, a * s + b * c
                parts.append((a, b))
            parts = small_fft(parts, -1.0)
            modes.append(
                (
                    jnp.concatenate([p[0] for p in parts], axis=1),
                    jnp.concatenate([p[1] for p in parts], axis=1),
                )
            )
        (ar, ai), (br, bi), (kr, ki), (pr, pi), (qr, qi) = modes
        inside = (jnp.abs(kx) <= limit) & (ky <= limit)

        def keep(values):
            return jnp.where(inside, dt * values, 0.0)

        (xr, xi), (yr, yi), (hr, hi) = state
        put(
            apply_parts(
                (
                    (xr + keep(ar + kx * ki), xi + keep(ai - kx * kr)),
                    (yr + keep(ky * ki - br), yi - keep(bi + ky * kr)),
                    (hr + keep(kx * pi + ky * qi), hi - keep(kx * pr + ky * qr)),
                ),
                factors,
                kx,
                ky,
            )
        )


def forward_x(datas, state, tables):
    group, _, _, kept, width = datas[0].shape
    count = len(datas)
    _, _, rows, grid_size = state.shape
    step = min(rows, 32)
    kept_steps = -(-kept // step)
    mat, tw = tables["fwd_x"]

    def kernel(*refs):
        forward_kernel(kept_steps, COURANT / grid_size, float(grid_size // 3), refs[:count], *refs[count:])

    return pl.pallas_call(
        kernel,
        grid=(rows // step,),
        in_specs=[
            *[
                pl.BlockSpec(
                    (group, 5, 2, step, width),
                    lambda i: (0, 0, 0, jnp.minimum(i, kept_steps - 1), 0),
                )
            ]
            * count,
            pl.BlockSpec((3, 2, step, grid_size), lambda i: (0, 0, i, 0)),
            pl.BlockSpec((3, step, grid_size), lambda i: (0, i, 0)),
            pl.BlockSpec((1, grid_size), lambda i: (0, 0)),
            pl.BlockSpec((step, 1), lambda i: (i, 0)),
            pl.BlockSpec(mat.shape, lambda i: (0, 0, 0)),
            pl.BlockSpec(tw.shape, lambda i: (0, 0, 0)),
        ],
        out_specs=pl.BlockSpec((3, 2, step, grid_size), lambda i: (0, 0, i, 0)),
        out_shape=jax.ShapeDtypeStruct(state.shape, jnp.float32),
        name="forward_x",
    )(*datas, state, tables["factors"], tables["kx"], tables["ky"], mat, tw)


def scan_kernel(data_ref, fac_ref, kx_ref, ky_ref, out_ref):
    kx, ky = kx_ref[...], ky_ref[...]
    factors = (fac_ref[0], fac_ref[1], fac_ref[2])
    carried = None
    for k in range(data_ref.shape[0]):
        new = tuple((data_ref[k, f, 0], data_ref[k, f, 1]) for f in range(3))
        if carried is not None:
            moved = apply_parts(carried, factors, kx, ky)
            new = tuple(
                (moved[f][0] + new[f][0], moved[f][1] + new[f][1]) for f in range(3)
            )
        for f in range(3):
            for c in range(2):
                out_ref[k, f, c] = new[f][c]
        carried = new


def slab_scan(data, factors, kx, ky):
    slabs, _, _, rows, grid_size = data.shape
    step = min(grid_size, 128)
    return pl.pallas_call(
        scan_kernel,
        grid=(grid_size // step,),
        in_specs=[
            pl.BlockSpec((slabs, 3, 2, rows, step), lambda i: (0, 0, 0, 0, i)),
            pl.BlockSpec((3, rows, step), lambda i: (0, 0, i)),
            pl.BlockSpec((1, step), lambda i: (0, i)),
            pl.BlockSpec((rows, 1), lambda i: (0, 0)),
        ],
        out_specs=pl.BlockSpec((slabs, 3, 2, rows, step), lambda i: (0, 0, 0, 0, i)),
        out_shape=jax.ShapeDtypeStruct(data.shape, jnp.float32),
        name="slab_scan",
    )(data, factors, kx, ky)


def make_tables(grid_size, rows, group, mine):
    counter = jnp.arange(grid_size, dtype=jnp.int32)
    kx = jnp.where(counter < grid_size // 2, counter, counter - grid_size).astype(jnp.float32)[None]
    ky = (group * jnp.arange(rows, dtype=jnp.int32) + mine).astype(jnp.float32)[:, None]
    kept = -(-(grid_size // 3 + 1) // group)
    kept = min(rows, -(-kept // 8) * 8)
    freq = (
        group * jnp.arange(rows, dtype=jnp.int32)[None]
        + jnp.arange(group, dtype=jnp.int32)[:, None]
    )
    turns = freq[:, :, None] * counter % grid_size
    angle = 2.0 * math.pi / grid_size * turns.astype(jnp.float32)
    waves = jnp.stack([jnp.cos(angle), -jnp.sin(angle)], axis=1)
    forward = (waves[:, :, :kept] / grid_size).reshape(group * 2 * kept, grid_size)
    turns = counter[:, None, None] * freq[None] % grid_size
    angle = 2.0 * math.pi / grid_size * turns.astype(jnp.float32)
    weight = jnp.where(freq == 0, 1.0, 2.0).astype(jnp.float32) / grid_size
    inverse = jnp.stack([weight * jnp.cos(angle), -weight * jnp.sin(angle)], axis=2)
    inverse = inverse.reshape(grid_size, group * 2 * rows)
    return {
        "group": group,
        "kx": kx,
        "ky": ky,
        "inv_y": table_pair(inverse),
        "fwd_y": table_pair(forward),
        "inv_x": lane_tables(grid_size, 1.0),
        "fwd_x": lane_tables(grid_size, -1.0),
        "factors": prop_factors(1.0, kx, ky, grid_size),
    }


def fine_step(state, tables):
    def exchange(values):
        return lax.all_to_all(values, GROUP, split_axis=0, concat_axis=0, tiled=True)

    landed = [exchange(part) for part in inverse_x(state, tables)]
    return forward_x([exchange(middle(part, tables)) for part in landed], state, tables)


def gathered(values, slabs, group, back):
    _, _, rows, grid_size = values.shape
    half = group // 2
    ident = lax.axis_index(SPACE)
    own = lax.axis_index(GROUP)
    per = rows // group
    shift = 0 if back else 1
    if back:
        pieces = values.reshape(3, 2, group, per, grid_size)
    else:
        pieces = values.reshape(3, 2, per, group, grid_size).transpose(3, 0, 1, 2, 4)

    landed = []
    for turn in range(group):
        links = []
        for slab in range(slabs):
            to_slab = (slab + shift) % slabs
            for z in range(group):
                q = (z + turn) % group
                far = (((to_slab // 2) * 2 + q // half) * 2 + to_slab % 2) * half + q % half
                near = slab * group + z
                links.append((far, near) if back else (near, far))
        if back:
            piece = lax.dynamic_index_in_dim(pieces, (own - turn) % group, 2, keepdims=False)
        else:
            piece = lax.dynamic_index_in_dim(pieces, (ident + turn) % group, 0, keepdims=False)
        landed.append(lax.ppermute(piece, EVERY, links))
    stacked = jnp.stack(landed)
    order = jnp.arange(group, dtype=jnp.int32)
    if back:
        stacked = jnp.take(stacked, (order - ident) % group, axis=0)
        return stacked.transpose(1, 2, 3, 0, 4).reshape(values.shape)
    stacked = jnp.take(stacked, (own - order) % group, axis=0)
    return stacked.transpose(1, 2, 0, 3, 4).reshape(values.shape)


def shards(c_state, init):
    rows, grid_size = c_state.shape[3:]
    group = lax.axis_size(SPACE)
    slabs = lax.axis_size(SLAB)
    own_slab = lax.axis_index(SLAB)
    tables = make_tables(grid_size, rows, group, lax.axis_index(GROUP))
    current = c_state[0]
    current = gathered(jnp.where(own_slab == slabs - 1, init, current), slabs, group, False)
    for _ in range(CF):
        current = fine_step(current, tables)
    per = rows // slabs
    start = lax.axis_index(SPACE) * rows + own_slab * per
    ky = (start + jnp.arange(per, dtype=jnp.int32)).astype(jnp.float32)[:, None]
    coarse = prop_factors(float(CF), tables["kx"], ky, grid_size)
    width = grid_size // STREAMS
    residuals, corrected, held = [], [], None
    for at in range(STREAMS):
        lane = slice(at * width, (at + 1) * width)
        part = current[..., lane]
        if held is not None:
            part, held = lax.optimization_barrier((part, held))
        held = gathered(part, slabs, group, True)
        residual = held - c_state[0, ..., lane]
        split = residual.reshape(3, 2, slabs, per, width).transpose(2, 0, 1, 3, 4)
        split = lax.all_to_all(split, SLAB, split_axis=0, concat_axis=0, tiled=True)
        split = slab_scan(split, coarse[..., lane], tables["kx"][:, lane], ky)
        split = lax.all_to_all(split, SLAB, split_axis=0, concat_axis=0, tiled=True)
        moved = split.transpose(1, 2, 0, 3, 4).reshape(residual.shape)
        residuals.append(residual)
        corrected.append(c_state[0, ..., lane] + moved)
    return (
        jnp.concatenate(corrected, axis=-1)[None],
        jnp.concatenate(residuals, axis=-1)[None],
    )


def solution(mesh):
    slabs, space = mesh.devices.shape
    fine = Mesh(mesh.devices.reshape(slabs // 2, 2, 2, space // 2), EVERY)
    spec = P(SLAB, None, None, SPACE, None)
    return jax.shard_map(
        shards,
        mesh=fine,
        in_specs=(spec, P(None, None, SPACE, None)),
        out_specs=(spec, spec),
        check_vma=False,
    )
```

```python
import math

import jax
import jax.numpy as jnp
import numpy as np
from jax import lax
from jax.experimental import pallas as pl
from jax.experimental.pallas import tpu as pltpu
from jax.sharding import Mesh, PartitionSpec as P

CF = 2
CORIOLIS = 1.0
HYPERDIFFUSION = 0.25
COURANT = 0.4
RADIX = 8
STREAMS = 2
SLAB = ("ta", "core")
SPACE = ("zh", "zl")
GROUP = ("core", "zl")
EVERY = ("ta", "core", "zh", "zl")


def split_pair(values):
    high = values.astype(jnp.bfloat16)
    return high, (values - high.astype(jnp.float32)).astype(jnp.bfloat16)


def table_pair(values):
    high = lax.reduce_precision(values, 8, 7)
    return jnp.stack([high, values - high]).astype(jnp.bfloat16)


def dot3(left, right):
    def one(a, b):
        return jnp.dot(a, b, preferred_element_type=jnp.float32)

    return one(left[0], right[0]) + (one(left[0], right[1]) + one(left[1], right[0]))


def small_fft(parts, sign):
    count = len(parts)
    if count == 1:
        return parts
    even = small_fft(parts[0::2], sign)
    odd = small_fft(parts[1::2], sign)
    low, high = [], []
    for k in range(count // 2):
        re, im = odd[k]
        if k == 0:
            tr, ti = re, im
        elif 4 * k == count:
            tr, ti = (-im, re) if sign > 0 else (im, -re)
        else:
            c = math.cos(2.0 * math.pi * k / count)
            s = sign * math.sin(2.0 * math.pi * k / count)
            tr, ti = re * c - im * s, re * s + im * c
        low.append((even[k][0] + tr, even[k][1] + ti))
        high.append((even[k][0] - tr, even[k][1] - ti))
    return low + high


def lane_tables(grid_size, sign):
    lanes = grid_size // RADIX
    n = np.arange(lanes)
    angle = 2.0 * np.pi * (n[:, None] * n[None, :] % lanes) / lanes
    c, s = np.cos(angle), sign * np.sin(angle)
    full = jnp.asarray(np.block([[c, s], [-s, c]]), jnp.float32)
    turn = 2.0 * np.pi * (np.arange(RADIX)[:, None] * n[None, :]) / grid_size
    twiddle = np.stack([np.cos(turn), sign * np.sin(turn)]).astype(np.float32)
    return table_pair(full), jnp.asarray(twiddle)


def prop_factors(steps, wave_x, wave_y, grid_size):
    time_step = COURANT / grid_size
    squared = wave_x * wave_x + wave_y * wave_y
    frequency = jnp.sqrt(CORIOLIS * CORIOLIS + squared)
    ratio = squared / (0.25 * grid_size * grid_size)
    log_damp = -HYPERDIFFUSION * (ratio * ratio) * (ratio * ratio)
    phase_angle = frequency * (steps * time_step)
    first_coef = jnp.sin(phase_angle) / frequency
    second_coef = (1.0 - jnp.cos(phase_angle)) / (frequency * frequency)
    damping = jnp.exp(steps * log_damp)
    return jnp.stack([first_coef, second_coef, damping])


def apply_parts(state, factors, kx, ky):
    first, second, damp = factors
    (xr, xi), (yr, yi), (hr, hi) = state
    done = []
    for x, y, p in ((xr, yr, -hi), (xi, yi, hr)):
        m1 = CORIOLIS * y - kx * p
        m2 = -CORIOLIS * x - ky * p
        m3 = kx * x + ky * y
        n1 = CORIOLIS * m2 - kx * m3
        n2 = -CORIOLIS * m1 - ky * m3
        n3 = kx * m1 + ky * m2
        done.append(
            (
                (x + first * m1 + second * n1) * damp,
                (y + first * m2 + second * n2) * damp,
                (p + first * m3 + second * n3) * damp,
            )
        )
    real, imag = done
    return ((real[0], imag[0]), (real[1], imag[1]), (imag[2], -real[2]))


def inverse_kernel(state_ref, kx_ref, ky_ref, mat_ref, tw_ref, *outs):
    kx, ky = kx_ref[...], ky_ref[...]
    lanes = mat_ref.shape[1] // 2
    width = outs[0].shape[4]
    chunk = width * len(outs)
    rows = ky.shape[0]
    matrix = (mat_ref[0], mat_ref[1])
    for f in range(4):
        if f < 3:
            re, im = state_ref[f, 0], state_ref[f, 1]
        else:
            re = ky * state_ref[0, 1] - kx * state_ref[1, 1]
            im = kx * state_ref[1, 0] - ky * state_ref[0, 0]
        parts = [
            (re[:, n * lanes : (n + 1) * lanes], im[:, n * lanes : (n + 1) * lanes])
            for n in range(RADIX)
        ]
        parts = small_fft(parts, 1.0)
        turned = []
        for k, (a, b) in enumerate(parts):
            if k > 0:
                c, s = tw_ref[0, k : k + 1], tw_ref[1, k : k + 1]
                a, b = a * c - b * s, a * s + b * c
            turned.append(jnp.concatenate([a, b], axis=1))
        made = dot3(split_pair(jnp.concatenate(turned, axis=0)), matrix)
        for k in range(RADIX):
            for c in range(2):
                block = made[k * rows : (k + 1) * rows, c * lanes : (c + 1) * lanes]
                if chunk >= lanes:
                    g, at = divmod(k * lanes, chunk)
                    o, at = divmod(at, width)
                    outs[o][g, f, c, :, at : at + lanes] = block
                else:
                    per = lanes // chunk
                    for i in range(per):
                        outs[0][k * per + i, f, c] = block[:, i * chunk : (i + 1) * chunk]


def inverse_x(state, tables):
    _, _, rows, grid_size = state.shape
    group = tables["group"]
    chunk = grid_size // group
    lanes = grid_size // RADIX
    count = 2 if chunk % (2 * lanes) == 0 else 1
    width = chunk // count
    step = min(rows, 32)
    mat, tw = tables["inv_x"]
    return pl.pallas_call(
        inverse_kernel,
        grid=(rows // step,),
        in_specs=[
            pl.BlockSpec((3, 2, step, grid_size), lambda i: (0, 0, i, 0)),
            pl.BlockSpec((1, grid_size), lambda i: (0, 0)),
            pl.BlockSpec((step, 1), lambda i: (i, 0)),
            pl.BlockSpec(mat.shape, lambda i: (0, 0, 0)),
            pl.BlockSpec(tw.shape, lambda i: (0, 0, 0)),
        ],
        out_specs=[pl.BlockSpec((group, 4, 2, step, width), lambda i: (0, 0, 0, i, 0))] * count,
        out_shape=[jax.ShapeDtypeStruct((group, 4, 2, rows, width), jnp.float32)] * count,
        name="inverse_x",
    )(state, tables["kx"], tables["ky"], mat, tw)


def middle_kernel(data_ref, inv_ref, fwd_ref, out_ref, high, low, total):
    at = pl.program_id(0)
    group, _, _, rows, chunk = data_ref.shape
    kept = out_ref.shape[3]

    @pl.when(at == 0)
    def _():
        for f in range(4):
            a, b = split_pair(data_ref[:, f].reshape(group * 2 * rows, chunk))
            high[:, f * chunk : (f + 1) * chunk] = a
            low[:, f * chunk : (f + 1) * chunk] = b

    made = dot3((inv_ref[0], inv_ref[1]), (high[...], low[...]))
    u, v, h, z = (made[:, f * chunk : (f + 1) * chunk] for f in range(4))
    products = (z * v, z * u, 0.5 * (u * u + v * v), h * u, h * v)
    term = dot3((fwd_ref[0], fwd_ref[1]), split_pair(jnp.concatenate(products, axis=1)))

    @pl.when(at == 0)
    def _():
        total[...] = term

    @pl.when(at > 0)
    def _():
        total[...] = total[...] + term

    @pl.when(at == pl.num_programs(0) - 1)
    def _():
        for f in range(5):
            field = total[:, f * chunk : (f + 1) * chunk]
            out_ref[:, f] = field.reshape(group, 2, kept, chunk)


def middle(data, tables):
    group, _, _, rows, chunk = data.shape
    inv, fwd = tables["inv_y"], tables["fwd_y"]
    grid_size = inv.shape[1]
    kept = fwd.shape[1] // (2 * group)
    step = grid_size // 4
    return pl.pallas_call(
        middle_kernel,
        grid=(grid_size // step,),
        in_specs=[
            pl.BlockSpec(data.shape, lambda i: (0, 0, 0, 0, 0)),
            pl.BlockSpec((2, step, inv.shape[2]), lambda i: (0, i, 0)),
            pl.BlockSpec((2, fwd.shape[1], step), lambda i: (0, 0, i)),
        ],
        out_specs=pl.BlockSpec((group, 5, 2, kept, chunk), lambda i: (0, 0, 0, 0, 0)),
        out_shape=jax.ShapeDtypeStruct((group, 5, 2, kept, chunk), jnp.float32),
        scratch_shapes=[
            pltpu.VMEM((group * 2 * rows, 4 * chunk), jnp.bfloat16),
            pltpu.VMEM((group * 2 * rows, 4 * chunk), jnp.bfloat16),
            pltpu.VMEM((group * 2 * kept, 5 * chunk), jnp.float32),
        ],
        compiler_params=pltpu.CompilerParams(vmem_limit_bytes=56 * 1024 * 1024),
        cost_estimate=pl.CostEstimate(
            flops=6 * grid_size * chunk * (4 * inv.shape[2] + 5 * fwd.shape[1]),
            bytes_accessed=4 * (inv.size + fwd.size + 2 * data.size),
            transcendentals=0,
        ),
        name="middle",
    )(data, inv, fwd)


def forward_kernel(kept_steps, dt, limit, datas, state_ref, fac_ref, kx_ref, ky_ref, mat_ref, tw_ref, out_ref):
    kx, ky = kx_ref[...], ky_ref[...]
    group, width = datas[0].shape[0], datas[0].shape[4]
    chunk = width * len(datas)
    rows = ky.shape[0]
    lanes = mat_ref.shape[1] // 2
    factors = (fac_ref[0], fac_ref[1], fac_ref[2])
    state = tuple((state_ref[f, 0], state_ref[f, 1]) for f in range(3))

    def put(values):
        for f in range(3):
            for c in range(2):
                out_ref[f, c] = values[f][c]

    @pl.when(pl.program_id(0) >= kept_steps)
    def _():
        put(apply_parts(state, factors, kx, ky))

    @pl.when(pl.program_id(0) < kept_steps)
    def _():
        matrix = (mat_ref[0], mat_ref[1])

        def piece(f, c, k):
            if chunk >= lanes:
                g, at = divmod(k * lanes, chunk)
                o, at = divmod(at, width)
                return datas[o][g, f, c, :, at : at + lanes]
            per = lanes // chunk
            return jnp.concatenate([datas[0][k * per + i, f, c] for i in range(per)], axis=1)

        stacked = jnp.concatenate(
            [
                jnp.concatenate([piece(f, 0, k), piece(f, 1, k)], axis=1)
                for f in range(5)
                for k in range(RADIX)
            ],
            axis=0,
        )
        made = dot3(split_pair(stacked), matrix)
        modes = []
        for f in range(5):
            parts = []
            for k in range(RADIX):
                start = (f * RADIX + k) * rows
                a = made[start : start + rows, :lanes]
                b = made[start : start + rows, lanes:]
                if k > 0:
                    c, s = tw_ref[0, k : k + 1], tw_ref[1, k : k + 1]
                    a, b = a * c - b * s, a * s + b * c
                parts.append((a, b))
            parts = small_fft(parts, -1.0)
            modes.append(
                (
                    jnp.concatenate([p[0] for p in parts], axis=1),
                    jnp.concatenate([p[1] for p in parts], axis=1),
                )
            )
        (ar, ai), (br, bi), (kr, ki), (pr, pi), (qr, qi) = modes
        inside = (jnp.abs(kx) <= limit) & (ky <= limit)

        def keep(values):
            return jnp.where(inside, dt * values, 0.0)

        (xr, xi), (yr, yi), (hr, hi) = state
        put(
            apply_parts(
                (
                    (xr + keep(ar + kx * ki), xi + keep(ai - kx * kr)),
                    (yr + keep(ky * ki - br), yi - keep(bi + ky * kr)),
                    (hr + keep(kx * pi + ky * qi), hi - keep(kx * pr + ky * qr)),
                ),
                factors,
                kx,
                ky,
            )
        )


def forward_x(datas, state, tables):
    group, _, _, kept, width = datas[0].shape
    count = len(datas)
    _, _, rows, grid_size = state.shape
    step = min(rows, 32)
    kept_steps = -(-kept // step)
    mat, tw = tables["fwd_x"]

    def kernel(*refs):
        forward_kernel(kept_steps, COURANT / grid_size, float(grid_size // 3), refs[:count], *refs[count:])

    return pl.pallas_call(
        kernel,
        grid=(rows // step,),
        in_specs=[
            *[
                pl.BlockSpec(
                    (group, 5, 2, step, width),
                    lambda i: (0, 0, 0, jnp.minimum(i, kept_steps - 1), 0),
                )
            ]
            * count,
            pl.BlockSpec((3, 2, step, grid_size), lambda i: (0, 0, i, 0)),
            pl.BlockSpec((3, step, grid_size), lambda i: (0, i, 0)),
            pl.BlockSpec((1, grid_size), lambda i: (0, 0)),
            pl.BlockSpec((step, 1), lambda i: (i, 0)),
            pl.BlockSpec(mat.shape, lambda i: (0, 0, 0)),
            pl.BlockSpec(tw.shape, lambda i: (0, 0, 0)),
        ],
        out_specs=pl.BlockSpec((3, 2, step, grid_size), lambda i: (0, 0, i, 0)),
        out_shape=jax.ShapeDtypeStruct(state.shape, jnp.float32),
        name="forward_x",
    )(*datas, state, tables["factors"], tables["kx"], tables["ky"], mat, tw)


def scan_kernel(data_ref, fac_ref, kx_ref, ky_ref, out_ref):
    kx, ky = kx_ref[...], ky_ref[...]
    factors = (fac_ref[0], fac_ref[1], fac_ref[2])
    carried = None
    for k in range(data_ref.shape[0]):
        new = tuple((data_ref[k, f, 0], data_ref[k, f, 1]) for f in range(3))
        if carried is not None:
            moved = apply_parts(carried, factors, kx, ky)
            new = tuple(
                (moved[f][0] + new[f][0], moved[f][1] + new[f][1]) for f in range(3)
            )
        for f in range(3):
            for c in range(2):
                out_ref[k, f, c] = new[f][c]
        carried = new


def slab_scan(data, factors, kx, ky):
    slabs, _, _, rows, grid_size = data.shape
    step = min(grid_size, 128)
    return pl.pallas_call(
        scan_kernel,
        grid=(grid_size // step,),
        in_specs=[
            pl.BlockSpec((slabs, 3, 2, rows, step), lambda i: (0, 0, 0, 0, i)),
            pl.BlockSpec((3, rows, step), lambda i: (0, 0, i)),
            pl.BlockSpec((1, step), lambda i: (0, i)),
            pl.BlockSpec((rows, 1), lambda i: (0, 0)),
        ],
        out_specs=pl.BlockSpec((slabs, 3, 2, rows, step), lambda i: (0, 0, 0, 0, i)),
        out_shape=jax.ShapeDtypeStruct(data.shape, jnp.float32),
        name="slab_scan",
    )(data, factors, kx, ky)


def make_tables(grid_size, rows, group, mine):
    counter = jnp.arange(grid_size, dtype=jnp.int32)
    kx = jnp.where(counter < grid_size // 2, counter, counter - grid_size).astype(jnp.float32)[None]
    ky = (group * jnp.arange(rows, dtype=jnp.int32) + mine).astype(jnp.float32)[:, None]
    kept = -(-(grid_size // 3 + 1) // group)
    kept = min(rows, -(-kept // 8) * 8)
    freq = (
        group * jnp.arange(rows, dtype=jnp.int32)[None]
        + jnp.arange(group, dtype=jnp.int32)[:, None]
    )
    turns = freq[:, :, None] * counter % grid_size
    angle = 2.0 * math.pi / grid_size * turns.astype(jnp.float32)
    waves = jnp.stack([jnp.cos(angle), -jnp.sin(angle)], axis=1)
    forward = (waves[:, :, :kept] / grid_size).reshape(group * 2 * kept, grid_size)
    turns = counter[:, None, None] * freq[None] % grid_size
    angle = 2.0 * math.pi / grid_size * turns.astype(jnp.float32)
    weight = jnp.where(freq == 0, 1.0, 2.0).astype(jnp.float32) / grid_size
    inverse = jnp.stack([weight * jnp.cos(angle), -weight * jnp.sin(angle)], axis=2)
    inverse = inverse.reshape(grid_size, group * 2 * rows)
    return {
        "group": group,
        "kx": kx,
        "ky": ky,
        "inv_y": table_pair(inverse),
        "fwd_y": table_pair(forward),
        "inv_x": lane_tables(grid_size, 1.0),
        "fwd_x": lane_tables(grid_size, -1.0),
        "factors": prop_factors(1.0, kx, ky, grid_size),
    }


def fine_step(state, tables):
    def exchange(values):
        return lax.all_to_all(values, GROUP, split_axis=0, concat_axis=0, tiled=True)

    landed = [exchange(part) for part in inverse_x(state, tables)]
    return forward_x([exchange(middle(part, tables)) for part in landed], state, tables)


def links_of(turn, slabs, group, back):
    half = group // 2
    shift = 0 if back else 1
    links = []
    for slab in range(slabs):
        to_slab = (slab + shift) % slabs
        for z in range(group):
            q = (z + turn) % group
            far = (((to_slab // 2) * 2 + q // half) * 2 + to_slab % 2) * half + q % half
            near = slab * group + z
            links.append((far, near) if back else (near, far))
    return links


def scalars(*values):
    return jnp.stack([jnp.asarray(v, jnp.int32) for v in values])


def whole_smem():
    return pl.BlockSpec(memory_space=pltpu.SMEM)


def deal(c_state, init, last, ident, group):
    _, _, _, rows, grid_size = c_state.shape
    per = rows // group

    def kernel(at_ref, c_ref, i_ref, *refs):
        outs, held, dealt = refs[:group], refs[group], refs[group + 1]

        tile = held.shape[2]

        @pl.when(at_ref[0] > 0)
        def _():
            for n in range(held.shape[0]):
                held[n] = i_ref[0, 0, :, n * tile : (n + 1) * tile]

        @pl.when(at_ref[0] == 0)
        def _():
            for n in range(held.shape[0]):
                held[n] = c_ref[0, 0, 0, :, n * tile : (n + 1) * tile]

        for q in range(group):
            for n in range(held.shape[0]):
                dealt[q, :, n * tile : (n + 1) * tile] = held[n, pl.ds(q, per, stride=group), :]
        for turn in range(group):
            outs[turn][0, 0] = dealt[lax.rem(at_ref[1] + turn, group)]

    return pl.pallas_call(
        kernel,
        grid=(3, 2),
        in_specs=[
            whole_smem(),
            pl.BlockSpec((1, 1, 1, rows, grid_size), lambda f, c: (0, f, c, 0, 0)),
            pl.BlockSpec((1, 1, rows, grid_size), lambda f, c: (f, c, 0, 0)),
        ],
        out_specs=[pl.BlockSpec((1, 1, per, grid_size), lambda f, c: (f, c, 0, 0))] * group,
        out_shape=[jax.ShapeDtypeStruct((3, 2, per, grid_size), jnp.float32)] * group,
        scratch_shapes=[
            pltpu.VMEM((grid_size // 128, rows, 128), jnp.float32),
            pltpu.VMEM((group, per, grid_size), jnp.float32),
        ],
        name="deal",
    )(scalars(last, ident), c_state, init)


def place(landed, own, group):
    _, _, per, grid_size = landed[0].shape

    def kernel(at_ref, *refs):
        out = refs[-1]
        for turn in range(group):
            z = lax.rem(at_ref[0] + (group - turn), group)
            out[0, 0, pl.ds(pl.multiple_of(z * per, 8), per)] = refs[turn][0, 0]

    return pl.pallas_call(
        kernel,
        grid=(3, 2),
        in_specs=[whole_smem()]
        + [pl.BlockSpec((1, 1, per, grid_size), lambda f, c: (f, c, 0, 0))] * group,
        out_specs=pl.BlockSpec((1, 1, per * group, grid_size), lambda f, c: (f, c, 0, 0)),
        out_shape=jax.ShapeDtypeStruct((3, 2, per * group, grid_size), jnp.float32),
        name="place",
    )(scalars(own), *landed)


def collect(landed, c_state, so_far, stream, slabs, ident):
    group = len(landed)
    _, _, per, width = landed[0].shape
    rows = per * group
    short = rows // slabs

    def kernel(at_ref, c_ref, *refs):
        residual, split, dealt, held = refs[-4:]
        for turn in range(group):
            dealt[lax.rem(at_ref[0] + turn, group)] = refs[turn][0, 0]
        for q in range(group):
            for n in range(held.shape[0]):
                held[n, pl.ds(q, per, stride=group), :] = dealt[q, :, n * 128 : (n + 1) * 128]
        for n in range(held.shape[0]):
            lanes = slice(n * 128, (n + 1) * 128)
            values = held[n] - c_ref[0, 0, 0, :, lanes]
            residual[0, 0, 0, :, lanes] = values
            for k in range(slabs):
                split[k, 0, 0, :, lanes] = values[k * short : (k + 1) * short]

    lane = pl.BlockSpec((1, 1, 1, rows, width), lambda f, c: (0, f, c, 0, stream))
    extra = [] if so_far is None else [so_far]
    return pl.pallas_call(
        kernel,
        grid=(3, 2),
        in_specs=[whole_smem(), lane]
        + [pl.BlockSpec((1, 1, per, width), lambda f, c: (f, c, 0, 0))] * group
        + [pl.BlockSpec(memory_space=pl.ANY)] * len(extra),
        out_specs=[
            lane,
            pl.BlockSpec((slabs, 1, 1, short, width), lambda f, c: (0, f, c, 0, 0)),
        ],
        out_shape=[
            jax.ShapeDtypeStruct(c_state.shape, jnp.float32),
            jax.ShapeDtypeStruct((slabs, 3, 2, short, width), jnp.float32),
        ],
        scratch_shapes=[
            pltpu.VMEM((group, per, width), jnp.float32),
            pltpu.VMEM((width // 128, rows, 128), jnp.float32),
        ],
        input_output_aliases={2 + group: 0} if extra else {},
        name="collect",
    )(scalars(ident), c_state, *landed, *extra)


def finish(moved, c_state):
    slabs, _, _, short, width = moved[0].shape
    rows, grid_size = c_state.shape[3:]

    def kernel(c_ref, *refs):
        out = refs[-1]
        for at in range(len(moved)):
            lane = slice(at * width, (at + 1) * width)
            for k in range(slabs):
                row = slice(k * short, (k + 1) * short)
                out[0, 0, 0, row, lane] = c_ref[0, 0, 0, row, lane] + refs[at][k, 0, 0]

    whole = pl.BlockSpec((1, 1, 1, rows, grid_size), lambda f, c: (0, f, c, 0, 0))
    return pl.pallas_call(
        kernel,
        grid=(3, 2),
        in_specs=[whole]
        + [pl.BlockSpec((slabs, 1, 1, short, width), lambda f, c: (0, f, c, 0, 0))] * len(moved),
        out_specs=whole,
        out_shape=jax.ShapeDtypeStruct(c_state.shape, jnp.float32),
        name="finish",
    )(c_state, *moved)


def gathered(values, slabs, group, back):
    _, _, rows, grid_size = values.shape
    ident = lax.axis_index(SPACE)
    own = lax.axis_index(GROUP)
    per = rows // group
    if back:
        pieces = values.reshape(3, 2, group, per, grid_size)
    else:
        pieces = values.reshape(3, 2, per, group, grid_size).transpose(3, 0, 1, 2, 4)

    landed = []
    for turn in range(group):
        links = links_of(turn, slabs, group, back)
        if back:
            piece = lax.dynamic_index_in_dim(pieces, (own - turn) % group, 2, keepdims=False)
        else:
            piece = lax.dynamic_index_in_dim(pieces, (ident + turn) % group, 0, keepdims=False)
        landed.append(lax.ppermute(piece, EVERY, links))
    stacked = jnp.stack(landed)
    order = jnp.arange(group, dtype=jnp.int32)
    if back:
        stacked = jnp.take(stacked, (order - ident) % group, axis=0)
        return stacked.transpose(1, 2, 3, 0, 4).reshape(values.shape)
    stacked = jnp.take(stacked, (own - order) % group, axis=0)
    return stacked.transpose(1, 2, 0, 3, 4).reshape(values.shape)


def shards(c_state, init):
    rows, grid_size = c_state.shape[3:]
    group = lax.axis_size(SPACE)
    slabs = lax.axis_size(SLAB)
    own_slab = lax.axis_index(SLAB)
    tables = make_tables(grid_size, rows, group, lax.axis_index(GROUP))
    aligned = rows // group % 8 == 0 and rows // slabs % 8 == 0
    ident = lax.axis_index(SPACE)
    last = own_slab == slabs - 1
    if aligned:
        pieces = deal(c_state, init, last, ident, group)
        landed = [
            lax.ppermute(piece, EVERY, links_of(turn, slabs, group, False))
            for turn, piece in enumerate(pieces)
        ]
        arrays = {key: tables[key] for key in ("inv_y", "fwd_y", "factors")}
        landed, arrays = lax.optimization_barrier((landed, arrays))
        tables.update(arrays)
        current = place(landed, lax.axis_index(GROUP), group)
    else:
        current = gathered(jnp.where(last, init, c_state[0]), slabs, group, False)
    for _ in range(CF):
        current = fine_step(current, tables)
    per = rows // slabs
    start = lax.axis_index(SPACE) * rows + own_slab * per
    ky = (start + jnp.arange(per, dtype=jnp.int32)).astype(jnp.float32)[:, None]
    coarse = prop_factors(float(CF), tables["kx"], ky, grid_size)
    width = grid_size // STREAMS
    if aligned:
        own = lax.axis_index(GROUP)
        short = rows // group
        landed, moved, residual = None, [], None
        for at in range(STREAMS):
            lane = slice(at * width, (at + 1) * width)
            part = current
            if landed is not None:
                part, landed = lax.optimization_barrier((current, landed))
            sent = [
                lax.dynamic_slice(
                    part,
                    (0, 0, (own - turn) % group * short, at * width),
                    (3, 2, short, width),
                )
                for turn in range(group)
            ]
            landed = [
                lax.ppermute(piece, EVERY, links_of(turn, slabs, group, True))
                for turn, piece in enumerate(sent)
            ]
            if moved:
                moved[-1] = lax.all_to_all(moved[-1], SLAB, split_axis=0, concat_axis=0, tiled=True)
                landed, moved[-1] = lax.optimization_barrier((landed, moved[-1]))
            residual, split = collect(landed, c_state, residual, at, slabs, ident)
            split = lax.all_to_all(split, SLAB, split_axis=0, concat_axis=0, tiled=True)
            moved.append(slab_scan(split, coarse[..., lane], tables["kx"][:, lane], ky))
        moved[-1] = lax.all_to_all(moved[-1], SLAB, split_axis=0, concat_axis=0, tiled=True)
        return (finish(moved, c_state), residual)
    residuals, corrected, held = [], [], None
    for at in range(STREAMS):
        lane = slice(at * width, (at + 1) * width)
        part = current[..., lane]
        if held is not None:
            part, held = lax.optimization_barrier((part, held))
        held = gathered(part, slabs, group, True)
        residual = held - c_state[0, ..., lane]
        split = residual.reshape(3, 2, slabs, per, width).transpose(2, 0, 1, 3, 4)
        split = lax.all_to_all(split, SLAB, split_axis=0, concat_axis=0, tiled=True)
        split = slab_scan(split, coarse[..., lane], tables["kx"][:, lane], ky)
        split = lax.all_to_all(split, SLAB, split_axis=0, concat_axis=0, tiled=True)
        moved = split.transpose(1, 2, 0, 3, 4).reshape(residual.shape)
        residuals.append(residual)
        corrected.append(c_state[0, ..., lane] + moved)
    return (
        jnp.concatenate(corrected, axis=-1)[None],
        jnp.concatenate(residuals, axis=-1)[None],
    )


def solution(mesh):
    slabs, space = mesh.devices.shape
    fine = Mesh(mesh.devices.reshape(slabs // 2, 2, 2, space // 2), EVERY)
    spec = P(SLAB, None, None, SPACE, None)
    return jax.shard_map(
        shards,
        mesh=fine,
        in_specs=(spec, P(None, None, SPACE, None)),
        out_specs=(spec, spec),
        check_vma=False,
    )
```
